32 devices in a mesh: rows: 16 (over z, y, x), width: 2 (over core).
Axes of the slice: x: 2, y: 2, z: 4, core: 2. Of those that a mesh axis runs over, the one named last changes fastest.
Arguments:
- left_feat: bfloat16 [16, 2048, 256], P('rows', 'width'), may hold values from -28 to 28
- right_feat: bfloat16 [16, 2048, 256], P('rows', 'width'), may hold values from -28 to 28
- refine_weight: bfloat16 [3, 3, 256, 256], replicated, may hold values from -0.125 to 0.125
Outputs:
- disparity: float32 [16, 2048], P('rows', 'width')
- refined: bfloat16 [16, 2048, 256], P('rows', 'width')
The draws below stay inside these ranges and needn't reach their ends.
All inputs are finite; a program needn't handle non-finite values.
Results may differ from the reference program's by a relative error of at most 0.0049.
Values may be sent and summed in bfloat16 or wider, within the bound.
A program may use at most 64 MiB of HBM per device.

```python
import math
import jax
import jax.numpy as jnp
from jax import lax

C = 256
W_DEV = 1024
ROWS = 16
W = 2048


def feature_pair(key):
    base = jax.random.fold_in(key, 911)
    key_right, key_noise, key_match = jax.random.split(base, 3)
    col_positions = jnp.arange(W, dtype=jnp.int32)
    shape = (ROWS, W, C)
    right_values = jax.random.truncated_normal(key_right, -4.0, 4.0, shape, jnp.float32)
    noise_values = jax.random.truncated_normal(key_noise, -4.0, 4.0, shape, jnp.float32)
    match_cols = jax.random.randint(key_match, (ROWS, W), 0, col_positions[None, :] + 1)
    gathered = jnp.take_along_axis(right_values, match_cols[:, :, None], axis=1)
    left_values = 0.7 * gathered + 0.7 * noise_values
    return (left_values.astype(jnp.bfloat16), right_values.astype(jnp.bfloat16))


def draw_left_feat(key, part):
    return feature_pair(key)[0]


def draw_right_feat(key, part):
    return feature_pair(key)[1]


def gaussian(own_key, dims, spread, most, kind=jnp.bfloat16):
    values = spread * jax.random.normal(own_key, dims, jnp.float32)
    return jnp.clip(values, min=-most, max=most).astype(kind)


def setup_inputs(seed: int = 0) -> dict:
    splits = jax.random.split(jax.random.key(seed), 4)
    left_feat = draw_left_feat(jax.random.fold_in(splits[3], 71), 0)
    right_feat = draw_right_feat(jax.random.fold_in(splits[3], 71), 0)
    refine_weight = gaussian(splits[2], (3, 3, C, C), (9 * C) ** -0.5, 0.125)
    return {"left_feat": left_feat, "right_feat": right_feat, "refine_weight": refine_weight}


NEG_FILL = -1e+30

def reference(left_feat, right_feat, refine_weight):
    n_rows, n_cols, chans = left_feat.shape
    score_scale = 1.0 / math.sqrt(chans)
    col_positions = jnp.arange(n_cols, dtype=jnp.int32)
    n_blocks = n_cols // W_DEV

    def one_block(index_pair):
        row_index, blk_index = index_pair
        queries = lax.dynamic_slice(left_feat, (row_index.astype(jnp.int32), (blk_index * W_DEV).astype(jnp.int32), jnp.int32(0)), (1, W_DEV, chans))[0]
        keys_row = lax.dynamic_index_in_dim(right_feat, row_index.astype(jnp.int32), 0, keepdims=False)
        query_positions = blk_index * W_DEV + jnp.arange(W_DEV, dtype=jnp.int32)
        scores = jnp.dot(queries, keys_row.T, preferred_element_type=jnp.float32) * score_scale
        allowed = col_positions[None, :] <= query_positions[:, None]
        scores = jnp.where(allowed, scores, NEG_FILL)
        row_max = scores.max(-1)
        weights = jnp.where(allowed, jnp.exp(scores - row_max[:, None]), 0.0)
        denominator = weights.sum(-1)
        matched = (jnp.dot(weights.astype(jnp.bfloat16), keys_row, preferred_element_type=jnp.float32) / denominator[:, None]).astype(jnp.bfloat16)
        expected = (weights * col_positions.astype(jnp.float32)[None, :]).sum(-1) / denominator
        return (matched, query_positions.astype(jnp.float32) - expected)
    row_ids = jnp.repeat(jnp.arange(n_rows, dtype=jnp.int32), n_blocks)
    blk_ids = jnp.tile(jnp.arange(n_blocks, dtype=jnp.int32), n_rows)
    matched, disparity = lax.map(one_block, (row_ids, blk_ids))
    matched = matched.reshape(n_rows, n_cols, chans)
    disparity = disparity.reshape(n_rows, n_cols)
    padded = jnp.pad(matched, ((1, 1), (1, 1), (0, 0)))
    total = jnp.zeros((n_rows * n_cols, chans), jnp.float32)
    for tap_row in range(3):
        for tap_col in range(3):
            window = padded[tap_row:tap_row + n_rows, tap_col:tap_col + n_cols].reshape(-1, chans)
            total = total + jnp.dot(window, refine_weight[tap_row, tap_col], preferred_element_type=jnp.float32)
    refined = total.reshape(n_rows, n_cols, chans).astype(jnp.bfloat16)
    return (disparity, refined)
```

```python
import functools
import math

import jax
import jax.numpy as jnp
from jax import lax
from jax.experimental import pallas as pl
from jax.experimental.pallas import tpu as pltpu
from jax.sharding import PartitionSpec as P

NEG_FILL = -1e30


def extended(value, sides, width):
    for axis, dim in sides:
        size, length = (lax.axis_size(axis), value.shape[dim])
        up = [(i, (i + 1) % size) for i in range(size - 1)]
        down = [(j, i) for i, j in up]
        last = lax.slice_in_dim(value, length - width, length, axis=dim)
        leading = lax.slice_in_dim(value, 0, width, axis=dim)
        before = lax.ppermute(last, axis, up)
        after = lax.ppermute(leading, axis, down)
        value = jnp.concatenate([before, value, after], axis=dim)
    return value


def absorb_block(state_now, query_rows, query_positions, sub_keys, key_positions):
    run_max, run_total, weighted, position_sum = state_now
    score_scale = 1.0 / math.sqrt(query_rows.shape[-1])
    scores = (
        jnp.einsum("rqc,rkc->rqk", query_rows, sub_keys, preferred_element_type=jnp.float32)
        * score_scale
    )
    allowed = (key_positions[None, :] <= query_positions[:, None]) & (key_positions[None, :] >= 0)
    scores = jnp.where(allowed[None], scores, NEG_FILL)
    new_max = jnp.maximum(run_max, scores.max(-1))
    factor = jnp.exp(run_max - new_max)
    weights = jnp.where(allowed[None], jnp.exp(scores - new_max[..., None]), 0.0)
    run_total = run_total * factor + weights.sum(-1)
    weighted = weighted * factor[..., None] + jnp.einsum(
        "rqk,rkc->rqc", weights.astype(jnp.bfloat16), sub_keys, preferred_element_type=jnp.float32
    )
    position_sum = position_sum * factor + (
        weights * key_positions.astype(jnp.float32)[None, None, :]
    ).sum(-1)
    return (new_max, run_total, weighted, position_sum)


def absorb_piece(state_now, query_rows, query_positions, key_piece):
    n_keys = key_piece.shape[1]
    sub_len = math.gcd(n_keys, 512)
    count = n_keys // sub_len
    last_query = query_positions[-1]

    def one_sub(carry_state, sub_index):
        sub_start = sub_index * sub_len
        sub_keys = lax.dynamic_slice_in_dim(key_piece, sub_index * sub_len, sub_len, 1)
        key_positions = sub_start + jnp.arange(sub_len, dtype=jnp.int32)
        result_state = lax.cond(
            sub_start <= last_query,
            lambda inner: absorb_block(inner, query_rows, query_positions, sub_keys, key_positions),
            lambda inner: inner,
            carry_state,
        )
        return (result_state, None)

    result, _ = lax.scan(one_sub, state_now, jnp.arange(count, dtype=jnp.int32))
    return result


def empty_state(rows_here, length, chans):
    return (
        jnp.full((rows_here, length), NEG_FILL, jnp.float32),
        jnp.zeros((rows_here, length), jnp.float32),
        jnp.zeros((rows_here, length, chans), jnp.float32),
        jnp.zeros((rows_here, length), jnp.float32),
    )


def finish_state(state_now, query_positions):
    run_max, run_total, weighted, position_sum = state_now
    matched = (weighted / run_total[..., None]).astype(jnp.bfloat16)
    disparity = query_positions.astype(jnp.float32)[None, :] - position_sum / run_total
    return (matched, disparity)


def body(left_feat, right_feat, refine_weight):
    rows_here, block_len, chans = left_feat.shape
    my_index = lax.axis_index("width")
    offset = my_index * block_len
    query_positions = offset + jnp.arange(block_len, dtype=jnp.int32)
    final_state = absorb_piece(
        empty_state(rows_here, block_len, chans),
        left_feat,
        query_positions,
        lax.all_gather(right_feat, "width", axis=1, tiled=True),
    )
    matched, disparity = finish_state(final_state, query_positions)
    padded = extended(matched, (("rows", 0), ("width", 1)), 1)
    total = jnp.zeros((rows_here * block_len, chans), jnp.float32)
    for tap_row in range(3):
        for tap_col in range(3):
            window = padded[tap_row : tap_row + rows_here, tap_col : tap_col + block_len].reshape(
                -1, chans
            )
            total = total + jnp.dot(
                window, refine_weight[tap_row, tap_col], preferred_element_type=jnp.float32
            )
    refined = total.reshape(rows_here, block_len, chans).astype(jnp.bfloat16)
    return (disparity, refined)


MESH = pl.DeviceIdType.MESH
EDGE = 16
LANES = 128


def attend(left, keys, scores, own, disp_ref, tile, first_key_tile, size):
    chans = left.shape[-1]
    gain = math.log2(math.e) / math.sqrt(chans)
    n_tiles = first_key_tile + tile + 1
    rows = pl.ds(tile * size, size)
    queries = left[rows, :]
    lane_max = jnp.full((size, LANES), NEG_FILL, jnp.float32)
    for kt in range(n_tiles):
        s = lax.dot_general(
            queries,
            keys[pl.ds(kt * size, size), :],
            (((1,), (1,)), ((), ())),
            preferred_element_type=jnp.float32,
        )
        if kt == n_tiles - 1:
            q_at = lax.broadcasted_iota(jnp.int32, (size, size), 0)
            k_at = lax.broadcasted_iota(jnp.int32, (size, size), 1)
            s = jnp.where(k_at <= q_at, s, NEG_FILL)
        scores[:, pl.ds(kt * size, size)] = s
        for c in range(0, size, LANES):
            lane_max = jnp.maximum(lane_max, s[:, c : c + LANES])
    row_max = jnp.max(lane_max, axis=1, keepdims=True)
    total = jnp.zeros((size, LANES), jnp.float32)
    prefix = jnp.zeros((size, LANES), jnp.float32)
    acc = jnp.zeros((size, chans), jnp.float32)
    for kt in range(n_tiles):
        p = jnp.exp2((scores[:, pl.ds(kt * size, size)] - row_max) * gain)
        for c in range(0, size, LANES):
            total = total + p[:, c : c + LANES]
            prefix = prefix + total
        acc = acc + jnp.dot(
            p.astype(jnp.bfloat16),
            keys[pl.ds(kt * size, size), :],
            preferred_element_type=jnp.float32,
        )
    denominator = jnp.sum(total, axis=1, keepdims=True)
    own[rows, :] = (acc * (1.0 / denominator)).astype(jnp.bfloat16)
    n_chunks = n_tiles * (size // LANES)
    lane = lax.broadcasted_iota(jnp.int32, (size, LANES), 1).astype(jnp.float32)
    position = LANES * (n_chunks * total - prefix) + lane * total
    total_t = jnp.sum(total.T, axis=0, keepdims=True)
    position_t = jnp.sum(position.T, axis=0, keepdims=True)
    at = lax.broadcasted_iota(jnp.int32, (1, size), 1) + (n_tiles - 1) * size
    disp_ref[:, rows] = at.astype(jnp.float32) - position_t / total_t


def kernel(
    n_rows, size, chunk,
    left_hbm, right_hbm, weight_hbm,
    disp_ref, out_ref,
    left, keys, weight, scores, own, arrived, edges, sums,
    load_sem, key_sem, x_sem, y_sem, z_sem, edge_sem,
):
    length, chans = left.shape
    n_tiles, n_chunks = length // size, length // chunk
    r, w = lax.axis_index("rows"), lax.axis_index("width")
    m = r % 4
    other_w = 1 - w
    x_row = r + 1 - 2 * (m % 2)
    y_row = r + 2 - 4 * (m // 2)
    outer = (m == 0) | (m == 3)
    below, above = outer & (r >= 4), outer & (r + 4 < n_rows)
    z_send = ((m == 0) & (r + 4 < n_rows)) | ((m == 3) & (r >= 4))
    z_recv = ((m == 0) & (r >= 4)) | ((m == 3) & (r + 4 < n_rows))
    z_row = jnp.where(m == 0, r + 4, jnp.where(m == 3, r - 4, x_row))

    loads = [
        pltpu.make_async_copy(left_hbm.at[0], left, load_sem.at[0]),
        pltpu.make_async_copy(right_hbm.at[0], keys.at[pl.ds(w * length, length)], load_sem.at[1]),
        pltpu.make_async_copy(weight_hbm, weight, load_sem.at[2]),
    ]
    for load in loads:
        load.start()

    barrier = pltpu.get_barrier_semaphore()
    for there in ((r, other_w), (x_row, w), (y_row, w)):
        pl.semaphore_signal(barrier, inc=1, device_id=there, device_id_type=MESH)

    @pl.when(below)
    def _():
        pl.semaphore_signal(barrier, inc=1, device_id=(r - 4, w), device_id_type=MESH)

    @pl.when(above)
    def _():
        pl.semaphore_signal(barrier, inc=1, device_id=(r + 4, w), device_id_type=MESH)

    pl.semaphore_wait(barrier, 3 + below.astype(jnp.int32) + above.astype(jnp.int32))

    def remote(src, dst, sems, k, row, col):
        return pltpu.make_async_remote_copy(
            src_ref=src, dst_ref=dst, send_sem=sems.at[0, k], recv_sem=sems.at[1, k],
            device_id=(row, col), device_id_type=MESH,
        )

    def part(k):
        return pl.ds(pl.multiple_of(k * chunk, chunk), chunk)

    def x_copy(k):
        return remote(own.at[part(k)], arrived.at[0, part(k)], x_sem, k, x_row, w)

    def y_copy(k):
        return remote(arrived.at[0, part(k)], arrived.at[1, part(k)], y_sem, k, y_row, w)

    def z_copy(k):
        return remote(arrived.at[1, part(k)], arrived.at[2, part(k)], z_sem, k, z_row, w)

    edge_at = pl.ds(pl.multiple_of((1 - w) * (length - EDGE), EDGE), EDGE)
    edge_chunk = (1 - w) * (n_chunks - 1)
    slot = jnp.where(outer, 2, 1)

    def edge_copy(j):
        src = own.at[edge_at] if j == 0 else arrived.at[0 if j == 1 else slot, edge_at]
        return remote(src, edges.at[j], edge_sem, j, r, other_w)

    key_copy = remote(right_hbm.at[0], keys.at[pl.ds(0, length)], key_sem, 0, r, other_w)

    @pl.when(w == 0)
    def _():
        key_copy.start()

    for load in loads:
        load.wait()

    for side in (0, 1):

        @pl.when(w == side)
        def _():
            if side == 1:
                key_copy.wait_recv()
            for tile in range(n_tiles):
                attend(left, keys, scores, own, disp_ref, tile, side * n_tiles, size)
                for k in range(tile * size // chunk, (tile + 1) * size // chunk):
                    x_copy(k).start()

    edge_copy(0).start()

    @pl.when(jnp.logical_not(z_recv))
    def _():
        arrived[2] = jnp.zeros((length, chans), jnp.bfloat16)

    zeros = jnp.zeros((EDGE, chans), jnp.float32)
    sums[0, pl.ds(0, EDGE), :] = zeros
    sums[2, pl.ds(EDGE + length, EDGE), :] = zeros
    x_tap = 2 - 2 * (m % 2)
    other_tap = 2 - x_tap

    def emit(start, n):
        before = sums[0, pl.ds(start + EDGE - 8, n + 8), :]
        after = sums[2, pl.ds(start + EDGE, n + 8), :]
        total = (
            pltpu.roll(before, 1, 0)[8:, :]
            + sums[1, pl.ds(start + EDGE, n), :]
            + pltpu.roll(after, n + 7, 0)[:n, :]
        )
        out_ref[0, pl.ds(start, n), :] = total.astype(jnp.bfloat16)

    def dots(value, tap):
        return [
            jnp.dot(value, weight[tap, b], preferred_element_type=jnp.float32) for b in range(3)
        ]

    def step(k, _):
        @pl.when(k < n_chunks)
        def _():
            x_copy(k).wait_recv()
            y_copy(k).start()

            @pl.when(k == edge_chunk)
            def _():
                edge_copy(1).start()

            first = dots(own[part(k), :], 1)
            second = dots(arrived[0, part(k), :], x_tap)
            for b in range(3):
                sums[b, pl.ds(pl.multiple_of(EDGE + k * chunk, EDGE), chunk), :] = first[b] + second[b]

        @pl.when((k >= 1) & (k < n_chunks + 1))
        def _():
            y_copy(k - 1).wait_recv()

            @pl.when(z_send)
            def _():
                z_copy(k - 1).start()

        @pl.when(k >= 2)
        def _():
            at = k - 2

            @pl.when(z_recv)
            def _():
                z_copy(at).wait_recv()

            @pl.when(at == edge_chunk)
            def _():
                edge_copy(2).start()

            third = dots(arrived[slot, part(at), :], other_tap)
            for b in range(3):
                here = pl.ds(pl.multiple_of(EDGE + at * chunk, EDGE), chunk)
                sums[b, here, :] = sums[b, here, :] + third[b]

            @pl.when(at >= 1)
            def _():
                emit(pl.multiple_of((at - 1) * chunk, chunk), chunk)

        return 0

    lax.fori_loop(0, n_chunks + 2, step, 0)

    for j in range(3):
        edge_copy(j).wait_recv()
    tap_col = 2 - 2 * w
    rim = (
        jnp.dot(edges[0], weight[1, tap_col], preferred_element_type=jnp.float32)
        + jnp.dot(edges[1], weight[x_tap, tap_col], preferred_element_type=jnp.float32)
        + jnp.dot(edges[2], weight[other_tap, tap_col], preferred_element_type=jnp.float32)
    )

    @pl.when(w == 0)
    def _():
        sums[2, pl.ds(EDGE + length, EDGE), :] = rim

    @pl.when(w == 1)
    def _():
        sums[0, pl.ds(0, EDGE), :] = rim
        emit(0, EDGE)

    emit(length - chunk, chunk)

    @pl.when(w == 0)
    def _():
        key_copy.wait_send()

    for j in range(3):
        edge_copy(j).wait_send()

    def drain(k, _):
        x_copy(k).wait_send()
        y_copy(k).wait_send()

        @pl.when(z_send)
        def _():
            z_copy(k).wait_send()

        return 0

    lax.fori_loop(0, n_chunks, drain, 0)


def fused(n_rows, left_feat, right_feat, refine_weight):
    _, length, chans = left_feat.shape
    size = math.gcd(length, 256)
    chunk = math.gcd(size, 128)
    n_chunks = length // chunk
    bf16, f32 = jnp.bfloat16, jnp.float32
    dma = pltpu.SemaphoreType.DMA
    return pl.pallas_call(
        functools.partial(kernel, n_rows, size, chunk),
        out_shape=(
            jax.ShapeDtypeStruct((1, length), f32),
            jax.ShapeDtypeStruct((1, length, chans), bf16),
        ),
        in_specs=[pl.BlockSpec(memory_space=pl.ANY)] * 3,
        out_specs=[pl.BlockSpec(memory_space=pltpu.VMEM)] * 2,
        scratch_shapes=[
            pltpu.VMEM((length, chans), bf16),
            pltpu.VMEM((2 * length, chans), bf16),
            pltpu.VMEM((3, 3, chans, chans), bf16),
            pltpu.VMEM((size, 2 * length), f32),
            pltpu.VMEM((length, chans), bf16),
            pltpu.VMEM((3, length, chans), bf16),
            pltpu.VMEM((3, EDGE, chans), bf16),
            pltpu.VMEM((3, length + 2 * EDGE, chans), f32),
            dma((3,)),
            dma((2, 1)),
            dma((2, n_chunks)),
            dma((2, n_chunks)),
            dma((2, n_chunks)),
            dma((2, 3)),
        ],
        compiler_params=pltpu.CompilerParams(collective_id=0, has_side_effects=True),
    )(left_feat, right_feat, refine_weight)


def solution(mesh):
    n_rows, n_width = mesh.shape["rows"], mesh.shape["width"]

    def local(left_feat, right_feat, refine_weight):
        rows_here, length, chans = left_feat.shape
        fits = n_rows % 4 == 0 and n_width == 2 and rows_here == 1
        if fits and length % LANES == 0 and chans % LANES == 0:
            return fused(n_rows, left_feat, right_feat, refine_weight)
        return body(left_feat, right_feat, refine_weight)

    placed = (P("rows", "width", None), P("rows", "width", None), P())
    return jax.shard_map(
        local,
        mesh=mesh,
        in_specs=placed,
        out_specs=(P("rows", "width"), P("rows", "width", None)),
        check_vma=False,
    )
```

```python
import functools
import math

import jax
import jax.numpy as jnp
from jax import lax
from jax.experimental import pallas as pl
from jax.experimental.pallas import tpu as pltpu
from jax.sharding import PartitionSpec as P

NEG_FILL = -1e30


def extended(value, sides, width):
    for axis, dim in sides:
        size, length = (lax.axis_size(axis), value.shape[dim])
        up = [(i, (i + 1) % size) for i in range(size - 1)]
        down = [(j, i) for i, j in up]
        last = lax.slice_in_dim(value, length - width, length, axis=dim)
        leading = lax.slice_in_dim(value, 0, width, axis=dim)
        before = lax.ppermute(last, axis, up)
        after = lax.ppermute(leading, axis, down)
        value = jnp.concatenate([before, value, after], axis=dim)
    return value


def absorb_block(state_now, query_rows, query_positions, sub_keys, key_positions):
    run_max, run_total, weighted, position_sum = state_now
    score_scale = 1.0 / math.sqrt(query_rows.shape[-1])
    scores = (
        jnp.einsum("rqc,rkc->rqk", query_rows, sub_keys, preferred_element_type=jnp.float32)
        * score_scale
    )
    allowed = (key_positions[None, :] <= query_positions[:, None]) & (key_positions[None, :] >= 0)
    scores = jnp.where(allowed[None], scores, NEG_FILL)
    new_max = jnp.maximum(run_max, scores.max(-1))
    factor = jnp.exp(run_max - new_max)
    weights = jnp.where(allowed[None], jnp.exp(scores - new_max[..., None]), 0.0)
    run_total = run_total * factor + weights.sum(-1)
    weighted = weighted * factor[..., None] + jnp.einsum(
        "rqk,rkc->rqc", weights.astype(jnp.bfloat16), sub_keys, preferred_element_type=jnp.float32
    )
    position_sum = position_sum * factor + (
        weights * key_positions.astype(jnp.float32)[None, None, :]
    ).sum(-1)
    return (new_max, run_total, weighted, position_sum)


def absorb_piece(state_now, query_rows, query_positions, key_piece):
    n_keys = key_piece.shape[1]
    sub_len = math.gcd(n_keys, 512)
    count = n_keys // sub_len
    last_query = query_positions[-1]

    def one_sub(carry_state, sub_index):
        sub_start = sub_index * sub_len
        sub_keys = lax.dynamic_slice_in_dim(key_piece, sub_index * sub_len, sub_len, 1)
        key_positions = sub_start + jnp.arange(sub_len, dtype=jnp.int32)
        result_state = lax.cond(
            sub_start <= last_query,
            lambda inner: absorb_block(inner, query_rows, query_positions, sub_keys, key_positions),
            lambda inner: inner,
            carry_state,
        )
        return (result_state, None)

    result, _ = lax.scan(one_sub, state_now, jnp.arange(count, dtype=jnp.int32))
    return result


def empty_state(rows_here, length, chans):
    return (
        jnp.full((rows_here, length), NEG_FILL, jnp.float32),
        jnp.zeros((rows_here, length), jnp.float32),
        jnp.zeros((rows_here, length, chans), jnp.float32),
        jnp.zeros((rows_here, length), jnp.float32),
    )


def finish_state(state_now, query_positions):
    run_max, run_total, weighted, position_sum = state_now
    matched = (weighted / run_total[..., None]).astype(jnp.bfloat16)
    disparity = query_positions.astype(jnp.float32)[None, :] - position_sum / run_total
    return (matched, disparity)


def body(left_feat, right_feat, refine_weight):
    rows_here, block_len, chans = left_feat.shape
    my_index = lax.axis_index("width")
    offset = my_index * block_len
    query_positions = offset + jnp.arange(block_len, dtype=jnp.int32)
    final_state = absorb_piece(
        empty_state(rows_here, block_len, chans),
        left_feat,
        query_positions,
        lax.all_gather(right_feat, "width", axis=1, tiled=True),
    )
    matched, disparity = finish_state(final_state, query_positions)
    padded = extended(matched, (("rows", 0), ("width", 1)), 1)
    total = jnp.zeros((rows_here * block_len, chans), jnp.float32)
    for tap_row in range(3):
        for tap_col in range(3):
            window = padded[tap_row : tap_row + rows_here, tap_col : tap_col + block_len].reshape(
                -1, chans
            )
            total = total + jnp.dot(
                window, refine_weight[tap_row, tap_col], preferred_element_type=jnp.float32
            )
    refined = total.reshape(rows_here, block_len, chans).astype(jnp.bfloat16)
    return (disparity, refined)


MESH = pl.DeviceIdType.MESH
EDGE = 16
LANES = 128
CHUNK = 128
Y_LAG = 2
Z_LAG = 4
TILE_LAG = (9, 9)


def attend(left, keys, scores, own, disp_ref, tile, first_key_tile, size):
    chans = left.shape[-1]
    gain = math.log2(math.e) / math.sqrt(chans)
    n_tiles = first_key_tile + tile + 1
    rows = pl.ds(tile * size, size)
    queries = left[rows, :]
    lane_max = jnp.full((size, LANES), NEG_FILL, jnp.float32)
    for kt in range(n_tiles):
        s = lax.dot_general(
            queries,
            keys[pl.ds(kt * size, size), :],
            (((1,), (1,)), ((), ())),
            preferred_element_type=jnp.float32,
        )
        if kt == n_tiles - 1:
            q_at = lax.broadcasted_iota(jnp.int32, (size, size), 0)
            k_at = lax.broadcasted_iota(jnp.int32, (size, size), 1)
            s = jnp.where(k_at <= q_at, s, NEG_FILL)
        scores[:, pl.ds(kt * size, size)] = s
        for c in range(0, size, LANES):
            lane_max = jnp.maximum(lane_max, s[:, c : c + LANES])
    row_max = jnp.max(lane_max, axis=1, keepdims=True)
    total = jnp.zeros((size, LANES), jnp.float32)
    prefix = jnp.zeros((size, LANES), jnp.float32)
    acc = jnp.zeros((size, chans), jnp.float32)
    for kt in range(n_tiles):
        p = jnp.exp2((scores[:, pl.ds(kt * size, size)] - row_max) * gain)
        for c in range(0, size, LANES):
            total = total + p[:, c : c + LANES]
            prefix = prefix + total
        acc = acc + jnp.dot(
            p.astype(jnp.bfloat16),
            keys[pl.ds(kt * size, size), :],
            preferred_element_type=jnp.float32,
        )
    denominator = jnp.sum(total, axis=1, keepdims=True)
    own[rows, :] = (acc * (1.0 / denominator)).astype(jnp.bfloat16)
    n_chunks = n_tiles * (size // LANES)
    lane = lax.broadcasted_iota(jnp.int32, (size, LANES), 1).astype(jnp.float32)
    position = LANES * (n_chunks * total - prefix) + lane * total
    total_t = jnp.sum(total.T, axis=0, keepdims=True)
    position_t = jnp.sum(position.T, axis=0, keepdims=True)
    at = lax.broadcasted_iota(jnp.int32, (1, size), 1) + (n_tiles - 1) * size
    disp_ref[:, rows] = at.astype(jnp.float32) - position_t / total_t


def kernel(
    n_rows, size, chunk,
    left_hbm, right_hbm, weight_hbm,
    disp_ref, out_ref,
    left, keys, weight, scores, own, arrived, edges, sums,
    load_sem, key_sem, x_sem, y_sem, z_sem, edge_sem,
):
    length, chans = left.shape
    n_tiles, n_chunks = length // size, length // chunk
    r, w = lax.axis_index("rows"), lax.axis_index("width")
    m = r % 4
    other_w = 1 - w
    x_row = r + 1 - 2 * (m % 2)
    y_row = r + 2 - 4 * (m // 2)
    outer = (m == 0) | (m == 3)
    below, above = outer & (r >= 4), outer & (r + 4 < n_rows)
    z_send = ((m == 0) & (r + 4 < n_rows)) | ((m == 3) & (r >= 4))
    z_recv = ((m == 0) & (r >= 4)) | ((m == 3) & (r + 4 < n_rows))
    z_row = jnp.where(m == 0, r + 4, jnp.where(m == 3, r - 4, x_row))

    loads = [
        pltpu.make_async_copy(left_hbm.at[0], left, load_sem.at[0]),
        pltpu.make_async_copy(right_hbm.at[0], keys.at[pl.ds(w * length, length)], load_sem.at[1]),
        pltpu.make_async_copy(weight_hbm, weight, load_sem.at[2]),
    ]
    for load in loads:
        load.start()

    barrier = pltpu.get_barrier_semaphore()
    for there in ((r, other_w), (x_row, w), (y_row, w)):
        pl.semaphore_signal(barrier, inc=1, device_id=there, device_id_type=MESH)

    @pl.when(below)
    def _():
        pl.semaphore_signal(barrier, inc=1, device_id=(r - 4, w), device_id_type=MESH)

    @pl.when(above)
    def _():
        pl.semaphore_signal(barrier, inc=1, device_id=(r + 4, w), device_id_type=MESH)

    pl.semaphore_wait(barrier, 3 + below.astype(jnp.int32) + above.astype(jnp.int32))

    def remote(src, dst, sems, k, row, col):
        return pltpu.make_async_remote_copy(
            src_ref=src, dst_ref=dst, send_sem=sems.at[0, k], recv_sem=sems.at[1, k],
            device_id=(row, col), device_id_type=MESH,
        )

    def part(k):
        return pl.ds(pl.multiple_of(k * chunk, chunk), chunk)

    def x_copy(k):
        return remote(own.at[part(k)], arrived.at[0, part(k)], x_sem, k, x_row, w)

    def y_copy(k):
        return remote(arrived.at[0, part(k)], arrived.at[1, part(k)], y_sem, k, y_row, w)

    def z_copy(k):
        return remote(arrived.at[1, part(k)], arrived.at[2, part(k)], z_sem, k, z_row, w)

    edge_at = pl.ds(pl.multiple_of((1 - w) * (length - EDGE), EDGE), EDGE)
    edge_chunk = (1 - w) * (n_chunks - 1)
    slot = jnp.where(outer, 2, 1)

    def edge_copy(j):
        src = own.at[edge_at] if j == 0 else arrived.at[0 if j == 1 else slot, edge_at]
        return remote(src, edges.at[j], edge_sem, j, r, other_w)

    key_copy = remote(right_hbm.at[0], keys.at[pl.ds(0, length)], key_sem, 0, r, other_w)

    @pl.when(w == 0)
    def _():
        key_copy.start()

    for load in loads:
        load.wait()

    @pl.when(jnp.logical_not(z_recv))
    def _():
        arrived[2] = jnp.zeros((length, chans), jnp.bfloat16)

    zeros = jnp.zeros((EDGE, chans), jnp.float32)
    sums[0, pl.ds(0, EDGE), :] = zeros
    sums[2, pl.ds(EDGE + length, EDGE), :] = zeros
    x_tap = 2 - 2 * (m % 2)
    other_tap = 2 - x_tap

    def emit(start, n):
        before = sums[0, pl.ds(start + EDGE - 8, n + 8), :]
        after = sums[2, pl.ds(start + EDGE, n + 8), :]
        total = (
            pltpu.roll(before, 1, 0)[8:, :]
            + sums[1, pl.ds(start + EDGE, n), :]
            + pltpu.roll(after, n + 7, 0)[:n, :]
        )
        out_ref[0, pl.ds(start, n), :] = total.astype(jnp.bfloat16)

    def dots(value, tap):
        return [
            jnp.dot(value, weight[tap, b], preferred_element_type=jnp.float32) for b in range(3)
        ]

    def step(k, _):
        @pl.when(k < n_chunks)
        def _():
            x_copy(k).wait_recv()
            y_copy(k).start()

            @pl.when(k == edge_chunk)
            def _():
                edge_copy(1).start()

            first = dots(own[part(k), :], 1)
            second = dots(arrived[0, part(k), :], x_tap)
            for b in range(3):
                sums[b, pl.ds(pl.multiple_of(EDGE + k * chunk, EDGE), chunk), :] = first[b] + second[b]

        @pl.when((k >= Y_LAG) & (k < n_chunks + Y_LAG))
        def _():
            y_copy(k - Y_LAG).wait_recv()

            @pl.when(z_send)
            def _():
                z_copy(k - Y_LAG).start()

        @pl.when(k >= Z_LAG)
        def _():
            at = k - Z_LAG

            @pl.when(z_recv)
            def _():
                z_copy(at).wait_recv()

            @pl.when(at == edge_chunk)
            def _():
                edge_copy(2).start()

            third = dots(arrived[slot, part(at), :], other_tap)
            for b in range(3):
                here = pl.ds(pl.multiple_of(EDGE + at * chunk, EDGE), chunk)
                sums[b, here, :] = sums[b, here, :] + third[b]

            @pl.when(at >= 1)
            def _():
                emit(pl.multiple_of((at - 1) * chunk, chunk), chunk)

        return 0

    per_tile = size // chunk
    for side in (0, 1):

        @pl.when(w == side)
        def _():
            done = 0
            if side == 1:
                key_copy.wait_recv()
            for tile in range(n_tiles):
                attend(left, keys, scores, own, disp_ref, tile, side * n_tiles, size)
                for k in range(tile * per_tile, (tile + 1) * per_tile):
                    x_copy(k).start()
                if tile == (1 - side) * (n_tiles - 1):
                    edge_copy(0).start()
                ready = max((tile - TILE_LAG[side]) * per_tile, done)
                if ready > done:
                    lax.fori_loop(done, ready, step, 0)
                done = ready
            lax.fori_loop(done, n_chunks + Z_LAG, step, 0)

    for j in range(3):
        edge_copy(j).wait_recv()
    tap_col = 2 - 2 * w
    rim = (
        jnp.dot(edges[0], weight[1, tap_col], preferred_element_type=jnp.float32)
        + jnp.dot(edges[1], weight[x_tap, tap_col], preferred_element_type=jnp.float32)
        + jnp.dot(edges[2], weight[other_tap, tap_col], preferred_element_type=jnp.float32)
    )

    @pl.when(w == 0)
    def _():
        sums[2, pl.ds(EDGE + length, EDGE), :] = rim

    @pl.when(w == 1)
    def _():
        sums[0, pl.ds(0, EDGE), :] = rim
        emit(0, EDGE)

    emit(length - chunk, chunk)

    @pl.when(w == 0)
    def _():
        key_copy.wait_send()

    for j in range(3):
        edge_copy(j).wait_send()

    def drain(k, _):
        x_copy(k).wait_send()
        y_copy(k).wait_send()

        @pl.when(z_send)
        def _():
            z_copy(k).wait_send()

        return 0

    lax.fori_loop(0, n_chunks, drain, 0)


def hand_on(disp_in, out_in, disp_ref, out_ref):
    disp_ref[...] = disp_in[...]
    out_ref[...] = out_in[...]


def fused(n_rows, left_feat, right_feat, refine_weight):
    _, length, chans = left_feat.shape
    size = math.gcd(length, 256)
    chunk = math.gcd(size, CHUNK)
    n_chunks = length // chunk
    bf16, f32 = jnp.bfloat16, jnp.float32
    dma = pltpu.SemaphoreType.DMA
    found = pl.pallas_call(
        functools.partial(kernel, n_rows, size, chunk),
        out_shape=(
            jax.ShapeDtypeStruct((1, length), f32),
            jax.ShapeDtypeStruct((1, length, chans), bf16),
        ),
        in_specs=[pl.BlockSpec(memory_space=pl.ANY)] * 3,
        out_specs=[pl.BlockSpec(memory_space=pltpu.VMEM)] * 2,
        scratch_shapes=[
            pltpu.VMEM((length, chans), bf16),
            pltpu.VMEM((2 * length, chans), bf16),
            pltpu.VMEM((3, 3, chans, chans), bf16),
            pltpu.VMEM((size, 2 * length), f32),
            pltpu.VMEM((length, chans), bf16),
            pltpu.VMEM((3, length, chans), bf16),
            pltpu.VMEM((3, EDGE, chans), bf16),
            pltpu.VMEM((3, length + 2 * EDGE, chans), f32),
            dma((3,)),
            dma((2, 1)),
            dma((2, n_chunks)),
            dma((2, n_chunks)),
            dma((2, n_chunks)),
            dma((2, 3)),
        ],
        compiler_params=pltpu.CompilerParams(collective_id=0, has_side_effects=True),
    )(left_feat, right_feat, refine_weight)
    return pl.pallas_call(
        hand_on,
        out_shape=tuple(jax.ShapeDtypeStruct(one.shape, one.dtype) for one in found),
        in_specs=[pl.BlockSpec(memory_space=pltpu.VMEM)] * 2,
        out_specs=[pl.BlockSpec(memory_space=pltpu.VMEM)] * 2,
    )(*found)


def solution(mesh):
    n_rows, n_width = mesh.shape["rows"], mesh.shape["width"]

    def local(left_feat, right_feat, refine_weight):
        rows_here, length, chans = left_feat.shape
        fits = n_rows % 4 == 0 and n_width == 2 and rows_here == 1
        if fits and length % LANES == 0 and chans % LANES == 0:
            return fused(n_rows, left_feat, right_feat, refine_weight)
        return body(left_feat, right_feat, refine_weight)

    placed = (P("rows", "width", None), P("rows", "width", None), P())
    return jax.shard_map(
        local,
        mesh=mesh,
        in_specs=placed,
        out_specs=(P("rows", "width"), P("rows", "width", None)),
        check_vma=False,
    )
```

```python
import functools
import math

import jax
import jax.numpy as jnp
from jax import lax
from jax.experimental import pallas as pl
from jax.experimental.pallas import tpu as pltpu
from jax.sharding import PartitionSpec as P

NEG_FILL = -1e30


def extended(value, sides, width):
    for axis, dim in sides:
        size, length = (lax.axis_size(axis), value.shape[dim])
        up = [(i, (i + 1) % size) for i in range(size - 1)]
        down = [(j, i) for i, j in up]
        last = lax.slice_in_dim(value, length - width, length, axis=dim)
        leading = lax.slice_in_dim(value, 0, width, axis=dim)
        before = lax.ppermute(last, axis, up)
        after = lax.ppermute(leading, axis, down)
        value = jnp.concatenate([before, value, after], axis=dim)
    return value


def absorb_block(state_now, query_rows, query_positions, sub_keys, key_positions):
    run_max, run_total, weighted, position_sum = state_now
    score_scale = 1.0 / math.sqrt(query_rows.shape[-1])
    scores = (
        jnp.einsum("rqc,rkc->rqk", query_rows, sub_keys, preferred_element_type=jnp.float32)
        * score_scale
    )
    allowed = (key_positions[None, :] <= query_positions[:, None]) & (key_positions[None, :] >= 0)
    scores = jnp.where(allowed[None], scores, NEG_FILL)
    new_max = jnp.maximum(run_max, scores.max(-1))
    factor = jnp.exp(run_max - new_max)
    weights = jnp.where(allowed[None], jnp.exp(scores - new_max[..., None]), 0.0)
    run_total = run_total * factor + weights.sum(-1)
    weighted = weighted * factor[..., None] + jnp.einsum(
        "rqk,rkc->rqc", weights.astype(jnp.bfloat16), sub_keys, preferred_element_type=jnp.float32
    )
    position_sum = position_sum * factor + (
        weights * key_positions.astype(jnp.float32)[None, None, :]
    ).sum(-1)
    return (new_max, run_total, weighted, position_sum)


def absorb_piece(state_now, query_rows, query_positions, key_piece):
    n_keys = key_piece.shape[1]
    sub_len = math.gcd(n_keys, 512)
    count = n_keys // sub_len
    last_query = query_positions[-1]

    def one_sub(carry_state, sub_index):
        sub_start = sub_index * sub_len
        sub_keys = lax.dynamic_slice_in_dim(key_piece, sub_index * sub_len, sub_len, 1)
        key_positions = sub_start + jnp.arange(sub_len, dtype=jnp.int32)
        result_state = lax.cond(
            sub_start <= last_query,
            lambda inner: absorb_block(inner, query_rows, query_positions, sub_keys, key_positions),
            lambda inner: inner,
            carry_state,
        )
        return (result_state, None)

    result, _ = lax.scan(one_sub, state_now, jnp.arange(count, dtype=jnp.int32))
    return result


def empty_state(rows_here, length, chans):
    return (
        jnp.full((rows_here, length), NEG_FILL, jnp.float32),
        jnp.zeros((rows_here, length), jnp.float32),
        jnp.zeros((rows_here, length, chans), jnp.float32),
        jnp.zeros((rows_here, length), jnp.float32),
    )


def finish_state(state_now, query_positions):
    run_max, run_total, weighted, position_sum = state_now
    matched = (weighted / run_total[..., None]).astype(jnp.bfloat16)
    disparity = query_positions.astype(jnp.float32)[None, :] - position_sum / run_total
    return (matched, disparity)


def body(left_feat, right_feat, refine_weight):
    rows_here, block_len, chans = left_feat.shape
    my_index = lax.axis_index("width")
    offset = my_index * block_len
    query_positions = offset + jnp.arange(block_len, dtype=jnp.int32)
    final_state = absorb_piece(
        empty_state(rows_here, block_len, chans),
        left_feat,
        query_positions,
        lax.all_gather(right_feat, "width", axis=1, tiled=True),
    )
    matched, disparity = finish_state(final_state, query_positions)
    padded = extended(matched, (("rows", 0), ("width", 1)), 1)
    total = jnp.zeros((rows_here * block_len, chans), jnp.float32)
    for tap_row in range(3):
        for tap_col in range(3):
            window = padded[tap_row : tap_row + rows_here, tap_col : tap_col + block_len].reshape(
                -1, chans
            )
            total = total + jnp.dot(
                window, refine_weight[tap_row, tap_col], preferred_element_type=jnp.float32
            )
    refined = total.reshape(rows_here, block_len, chans).astype(jnp.bfloat16)
    return (disparity, refined)


MESH = pl.DeviceIdType.MESH
EDGE = 16
LANES = 128
CHUNK = 64
Y_LAG = 6
Z_LAG = 12
TILE_LAG = (9, 9)


def attend(left, keys, scores, own, disp_ref, tile, first_key_tile, size):
    chans = left.shape[-1]
    gain = math.log2(math.e) / math.sqrt(chans)
    n_tiles = first_key_tile + tile + 1
    rows = pl.ds(tile * size, size)
    queries = left[rows, :]
    lane_max = jnp.full((size, LANES), NEG_FILL, jnp.float32)
    for kt in range(n_tiles):
        s = lax.dot_general(
            queries,
            keys[pl.ds(kt * size, size), :],
            (((1,), (1,)), ((), ())),
            preferred_element_type=jnp.float32,
        )
        if kt == n_tiles - 1:
            q_at = lax.broadcasted_iota(jnp.int32, (size, size), 0)
            k_at = lax.broadcasted_iota(jnp.int32, (size, size), 1)
            s = jnp.where(k_at <= q_at, s, NEG_FILL)
        scores[:, pl.ds(kt * size, size)] = s
        for c in range(0, size, LANES):
            lane_max = jnp.maximum(lane_max, s[:, c : c + LANES])
    row_max = jnp.max(lane_max, axis=1, keepdims=True)
    total = jnp.zeros((size, LANES), jnp.float32)
    prefix = jnp.zeros((size, LANES), jnp.float32)
    acc = jnp.zeros((size, chans), jnp.float32)
    for kt in range(n_tiles):
        p = jnp.exp2((scores[:, pl.ds(kt * size, size)] - row_max) * gain)
        for c in range(0, size, LANES):
            total = total + p[:, c : c + LANES]
            prefix = prefix + total
        acc = acc + jnp.dot(
            p.astype(jnp.bfloat16),
            keys[pl.ds(kt * size, size), :],
            preferred_element_type=jnp.float32,
        )
    denominator = jnp.sum(total, axis=1, keepdims=True)
    own[rows, :] = (acc * (1.0 / denominator)).astype(jnp.bfloat16)
    n_chunks = n_tiles * (size // LANES)
    lane = lax.broadcasted_iota(jnp.int32, (size, LANES), 1).astype(jnp.float32)
    position = LANES * (n_chunks * total - prefix) + lane * total
    total_t = jnp.sum(total.T, axis=0, keepdims=True)
    position_t = jnp.sum(position.T, axis=0, keepdims=True)
    at = lax.broadcasted_iota(jnp.int32, (1, size), 1) + (n_tiles - 1) * size
    disp_ref[:, rows] = at.astype(jnp.float32) - position_t / total_t


def kernel(
    n_rows, size, chunk,
    left_hbm, right_hbm, weight_hbm,
    disp_ref, out_ref,
    left, keys, weight, scores, own, arrived, edges, sums,
    load_sem, key_sem, x_sem, y_sem, z_sem, edge_sem,
):
    length, chans = left.shape
    n_tiles, n_chunks = length // size, length // chunk
    r, w = lax.axis_index("rows"), lax.axis_index("width")
    m = r % 4
    other_w = 1 - w
    x_row = r + 1 - 2 * (m % 2)
    y_row = r + 2 - 4 * (m // 2)
    outer = (m == 0) | (m == 3)
    below, above = outer & (r >= 4), outer & (r + 4 < n_rows)
    z_send = ((m == 0) & (r + 4 < n_rows)) | ((m == 3) & (r >= 4))
    z_recv = ((m == 0) & (r >= 4)) | ((m == 3) & (r + 4 < n_rows))
    z_row = jnp.where(m == 0, r + 4, jnp.where(m == 3, r - 4, x_row))

    loads = [
        pltpu.make_async_copy(left_hbm.at[0], left, load_sem.at[0]),
        pltpu.make_async_copy(right_hbm.at[0], keys.at[pl.ds(w * length, length)], load_sem.at[1]),
        pltpu.make_async_copy(weight_hbm, weight, load_sem.at[2]),
    ]
    for load in loads[:2]:
        load.start()

    barrier = pltpu.get_barrier_semaphore()
    for there in ((r, other_w), (x_row, w), (y_row, w)):
        pl.semaphore_signal(barrier, inc=1, device_id=there, device_id_type=MESH)

    @pl.when(below)
    def _():
        pl.semaphore_signal(barrier, inc=1, device_id=(r - 4, w), device_id_type=MESH)

    @pl.when(above)
    def _():
        pl.semaphore_signal(barrier, inc=1, device_id=(r + 4, w), device_id_type=MESH)

    pl.semaphore_wait(barrier, 3 + below.astype(jnp.int32) + above.astype(jnp.int32))

    def remote(src, dst, sems, k, row, col):
        return pltpu.make_async_remote_copy(
            src_ref=src, dst_ref=dst, send_sem=sems.at[0, k], recv_sem=sems.at[1, k],
            device_id=(row, col), device_id_type=MESH,
        )

    def part(k):
        return pl.ds(pl.multiple_of(k * chunk, chunk), chunk)

    def x_copy(k):
        return remote(own.at[part(k)], arrived.at[0, part(k)], x_sem, k, x_row, w)

    def y_copy(k):
        return remote(arrived.at[0, part(k)], arrived.at[1, part(k)], y_sem, k, y_row, w)

    def z_copy(k):
        return remote(arrived.at[1, part(k)], arrived.at[2, part(k)], z_sem, k, z_row, w)

    edge_at = pl.ds(pl.multiple_of((1 - w) * (length - EDGE), EDGE), EDGE)
    edge_chunk = (1 - w) * (n_chunks - 1)
    slot = jnp.where(outer, 2, 1)

    def edge_copy(j):
        src = own.at[edge_at] if j == 0 else arrived.at[0 if j == 1 else slot, edge_at]
        return remote(src, edges.at[j], edge_sem, j, r, other_w)

    key_copy = remote(right_hbm.at[0], keys.at[pl.ds(0, length)], key_sem, 0, r, other_w)

    @pl.when(w == 0)
    def _():
        key_copy.start()

    for load in loads[:2]:
        load.wait()
    loads[2].start()

    @pl.when(jnp.logical_not(z_recv))
    def _():
        arrived[2] = jnp.zeros((length, chans), jnp.bfloat16)

    zeros = jnp.zeros((EDGE, chans), jnp.float32)
    sums[0, pl.ds(0, EDGE), :] = zeros
    sums[2, pl.ds(EDGE + length, EDGE), :] = zeros
    x_tap = 2 - 2 * (m % 2)
    other_tap = 2 - x_tap

    def emit(start, n):
        before = sums[0, pl.ds(start + EDGE - 8, n + 8), :]
        after = sums[2, pl.ds(start + EDGE, n + 8), :]
        total = (
            pltpu.roll(before, 1, 0)[8:, :]
            + sums[1, pl.ds(start + EDGE, n), :]
            + pltpu.roll(after, n + 7, 0)[:n, :]
        )
        out_ref[0, pl.ds(start, n), :] = total.astype(jnp.bfloat16)

    def dots(value, tap):
        return [
            jnp.dot(value, weight[tap, b], preferred_element_type=jnp.float32) for b in range(3)
        ]

    def step(k, _):
        @pl.when(k < n_chunks)
        def _():
            x_copy(k).wait_recv()
            y_copy(k).start()

            @pl.when(k == edge_chunk)
            def _():
                edge_copy(1).start()

            first = dots(own[part(k), :], 1)
            second = dots(arrived[0, part(k), :], x_tap)
            for b in range(3):
                sums[b, pl.ds(pl.multiple_of(EDGE + k * chunk, EDGE), chunk), :] = first[b] + second[b]

        @pl.when((k >= Y_LAG) & (k < n_chunks + Y_LAG))
        def _():
            y_copy(k - Y_LAG).wait_recv()

            @pl.when(z_send)
            def _():
                z_copy(k - Y_LAG).start()

        @pl.when(k >= Z_LAG)
        def _():
            at = k - Z_LAG

            @pl.when(z_recv)
            def _():
                z_copy(at).wait_recv()

            @pl.when(at == edge_chunk)
            def _():
                edge_copy(2).start()

            third = dots(arrived[slot, part(at), :], other_tap)
            for b in range(3):
                here = pl.ds(pl.multiple_of(EDGE + at * chunk, EDGE), chunk)
                sums[b, here, :] = sums[b, here, :] + third[b]

            @pl.when(at >= 1)
            def _():
                emit(pl.multiple_of((at - 1) * chunk, chunk), chunk)

        return 0

    per_tile = size // chunk
    for side in (0, 1):

        @pl.when(w == side)
        def _():
            done = 0
            if side == 1:
                key_copy.wait_recv()
            for tile in range(n_tiles):
                attend(left, keys, scores, own, disp_ref, tile, side * n_tiles, size)
                for k in range(tile * per_tile, (tile + 1) * per_tile):
                    x_copy(k).start()
                if tile == (1 - side) * (n_tiles - 1):
                    edge_copy(0).start()
                if tile == 0:
                    loads[2].wait()
                ready = max((tile - TILE_LAG[side]) * per_tile, done)
                if ready > done:
                    lax.fori_loop(done, ready, step, 0)
                done = ready
            lax.fori_loop(done, n_chunks + Z_LAG, step, 0)

    for j in range(3):
        edge_copy(j).wait_recv()
    tap_col = 2 - 2 * w
    rim = (
        jnp.dot(edges[0], weight[1, tap_col], preferred_element_type=jnp.float32)
        + jnp.dot(edges[1], weight[x_tap, tap_col], preferred_element_type=jnp.float32)
        + jnp.dot(edges[2], weight[other_tap, tap_col], preferred_element_type=jnp.float32)
    )

    @pl.when(w == 0)
    def _():
        sums[2, pl.ds(EDGE + length, EDGE), :] = rim

    @pl.when(w == 1)
    def _():
        sums[0, pl.ds(0, EDGE), :] = rim
        emit(0, EDGE)

    emit(length - chunk, chunk)

    @pl.when(w == 0)
    def _():
        key_copy.wait_send()

    for j in range(3):
        edge_copy(j).wait_send()

    def drain(k, _):
        x_copy(k).wait_send()
        y_copy(k).wait_send()

        @pl.when(z_send)
        def _():
            z_copy(k).wait_send()

        return 0

    lax.fori_loop(0, n_chunks, drain, 0)


def hand_on(disp_in, out_in, disp_ref, out_ref):
    disp_ref[...] = disp_in[...]
    out_ref[...] = out_in[...]


def fused(n_rows, left_feat, right_feat, refine_weight):
    _, length, chans = left_feat.shape
    size = math.gcd(length, 256)
    chunk = math.gcd(size, CHUNK)
    n_chunks = length // chunk
    bf16, f32 = jnp.bfloat16, jnp.float32
    dma = pltpu.SemaphoreType.DMA
    found = pl.pallas_call(
        functools.partial(kernel, n_rows, size, chunk),
        out_shape=(
            jax.ShapeDtypeStruct((1, length), f32),
            jax.ShapeDtypeStruct((1, length, chans), bf16),
        ),
        in_specs=[pl.BlockSpec(memory_space=pl.ANY)] * 3,
        out_specs=[pl.BlockSpec(memory_space=pltpu.VMEM)] * 2,
        scratch_shapes=[
            pltpu.VMEM((length, chans), bf16),
            pltpu.VMEM((2 * length, chans), bf16),
            pltpu.VMEM((3, 3, chans, chans), bf16),
            pltpu.VMEM((size, 2 * length), f32),
            pltpu.VMEM((length, chans), bf16),
            pltpu.VMEM((3, length, chans), bf16),
            pltpu.VMEM((3, EDGE, chans), bf16),
            pltpu.VMEM((3, length + 2 * EDGE, chans), f32),
            dma((3,)),
            dma((2, 1)),
            dma((2, n_chunks)),
            dma((2, n_chunks)),
            dma((2, n_chunks)),
            dma((2, 3)),
        ],
        compiler_params=pltpu.CompilerParams(collective_id=0, has_side_effects=True),
    )(left_feat, right_feat, refine_weight)
    return pl.pallas_call(
        hand_on,
        out_shape=tuple(jax.ShapeDtypeStruct(one.shape, one.dtype) for one in found),
        in_specs=[pl.BlockSpec(memory_space=pltpu.VMEM)] * 2,
        out_specs=[pl.BlockSpec(memory_space=pltpu.VMEM)] * 2,
    )(*found)


def solution(mesh):
    n_rows, n_width = mesh.shape["rows"], mesh.shape["width"]

    def local(left_feat, right_feat, refine_weight):
        rows_here, length, chans = left_feat.shape
        fits = n_rows % 4 == 0 and n_width == 2 and rows_here == 1
        if fits and length % LANES == 0 and chans % LANES == 0:
            return fused(n_rows, left_feat, right_feat, refine_weight)
        return body(left_feat, right_feat, refine_weight)

    placed = (P("rows", "width", None), P("rows", "width", None), P())
    return jax.shard_map(
        local,
        mesh=mesh,
        in_specs=placed,
        out_specs=(P("rows", "width"), P("rows", "width", None)),
        check_vma=False,
    )
```
